256 devices in a mesh: req: 64 (over x, z, y_hi), tp: 4 (over y_lo, core).
Axes of the slice: x: 4, y: 4 (y_hi: 2, y_lo: 2; y = y_hi * 2 + y_lo), z: 8, core: 2. Of those that a mesh axis runs over, the one named last changes fastest.
Arguments:
- queries: bfloat16 [8192, 2048], P('req', 'tp'), may hold values from -8 to 8
- new_kv: bfloat16 [4, 8192, 256], P('tp', 'req'), may hold values from -20 to 20
- prefix_kv: bfloat16 [4, 16384, 256], P('tp', 'req'), may hold values from -8 to 8
- cache_kv: bfloat16 [4, 3072, 128, 256], P('tp', 'req'), may hold values from -6 to 6
- page_table: int32 [64, 48], P('req'), may hold values from 0 to 47, each once within a row
- page_counts: int32 [64, 2], P('req'), may hold values from 1 to 32, as said below
- cache_slack: int32 [64, 2], P('req'), may hold values from 0 to 127
- parents: int32 [128, 64], P('req'), may hold values from 0 to 62, as said below
- tree_sizes: int32 [128], P('req'), may hold values from 32 to 64, as said below
- accepted: int32 [128], P('req'), may hold values from 0 to 63, as said below
- out_weight: bfloat16 [2048, 4096], P('tp'), may hold values from -0.5 to 0.5
- residual: bfloat16 [8192, 4096], P(('req', 'tp')), may hold values from -20 to 20
- norm_gain: bfloat16 [4096], replicated, may hold values from 0.5 to 1.5
Outputs:
- hidden_state: bfloat16 [8192, 4096], P(('req', 'tp'))
- normed_state: bfloat16 [8192, 4096], P(('req', 'tp'))
- accepted_kv: bfloat16 [4, 8192, 256], P('tp', 'req')
The draws below stay inside these ranges and needn't reach their ends.
Inputs may be any that keep to these rules, and one draw needn't show every extreme that they name: `page_table`: each row lists every page of one req index's pool once. `page_counts`: the 2 counts of one req index sum to 48, and exactly one of them is 32. `parents`: slot 0 of every tree names 0; slot i >= 1 names a slot below i. Slots 0 to tree_sizes - 1 of a request form its tree; its other slots are unused. `accepted`: a slot of its request's tree.
All inputs are finite; a program needn't handle non-finite values.
Results may differ from the reference program's by a relative error of at most 0.012.
Values may be sent and summed in bfloat16 or wider, within the bound.
No kernel may reach another device: no remote copies, remote signals or barrier semaphores. Data moves between devices by JAX's collectives and lax.ppermute only.
A program may use at most 192 MiB of HBM per device.

```python
import math
import jax
import jax.numpy as jnp
from jax import lax

D = 4096
KVH = 4
HD = 128
HEADS = 16
PAGE = 128
MAXP = 32
DRAFT = 64
REQ_DEV = 2
P_DEV = 48
POOL = 3072
PREFIX = 16384
REQUESTS = 128
TOKENS = 8192
N_REQ = 64


def tree_counts(key):
    counted = jax.random.randint(jax.random.fold_in(key, 5), (REQUESTS,), DRAFT // 2, DRAFT + 1)
    return counted.at[0].set(DRAFT).astype(jnp.int32)


def draw_page_counts(key, part):
    half_pages = MAXP // 2
    paired = (REQ_DEV - 1) // 2
    deltas = jax.random.randint(jax.random.fold_in(key, 22), (N_REQ, paired), 1 - half_pages, half_pages)
    lone = jnp.zeros((N_REQ, (REQ_DEV - 1) % 2), jnp.int32)
    others = jnp.concatenate([deltas, -deltas, lone], axis=1) + half_pages
    full = jnp.concatenate([jnp.full((N_REQ, 1), MAXP, jnp.int32), others.astype(jnp.int32)], axis=1)
    row_keys = jax.random.split(jax.random.fold_in(key, 21), N_REQ)
    mixed = jax.vmap(lambda row_key, row: jax.random.permutation(row_key, row))(row_keys, full)
    return mixed.astype(jnp.int32)


def draw_queries(key, part):
    base = jnp.clip(jax.random.normal(jax.random.fold_in(key, 1), (TOKENS, HEADS * HD), jnp.float32) * 1.5, -8.0, 8.0)
    return base.astype(jnp.bfloat16)


def draw_prefix_kv(key, part):
    base = jnp.clip(jax.random.normal(jax.random.fold_in(key, 2), (KVH, PREFIX, 2 * HD), jnp.float32), -6.0, 6.0)
    return base.astype(jnp.bfloat16)


def draw_residual(key, part):
    row_scale = jnp.exp(jax.random.uniform(jax.random.fold_in(key, 3), (TOKENS, 1), jnp.float32, math.log(0.15), math.log(1.5)))
    column_scale = jnp.exp(jax.random.uniform(jax.random.fold_in(key, 4), (1, D), jnp.float32, math.log(0.3), math.log(3.0)))
    normal_part = jnp.clip(jax.random.normal(jax.random.fold_in(key, 8), (TOKENS, D), jnp.float32), -4.0, 4.0)
    return (normal_part * row_scale * column_scale).astype(jnp.bfloat16)


def draw_parents(key, part):
    slot_index = jnp.arange(DRAFT, dtype=jnp.int32)
    upper = jnp.maximum(slot_index, 1)[None, :]
    drawn_parent = jax.random.randint(jax.random.fold_in(key, 7), (REQUESTS, DRAFT), 0, upper)
    drawn_parent = drawn_parent.at[0, DRAFT - 1].set(DRAFT - 2)
    return drawn_parent.astype(jnp.int32)


def draw_tree_sizes(key, part):
    return tree_counts(key)


def draw_accepted(key, part):
    counted = tree_counts(key)
    chosen = jax.random.randint(jax.random.fold_in(key, 6), (REQUESTS,), 0, counted)
    return chosen.at[0].set(DRAFT - 1).astype(jnp.int32)


def set_ends(values, own_key, least, high):
    index_at = [jax.random.randint(jax.random.fold_in(own_key, axis), (), 0, length) for axis, length in enumerate(values.shape)]
    widest = values.shape.index(max(values.shape))
    beside = index_at[:widest] + [(index_at[widest] + 1) % values.shape[widest]] + index_at[widest + 1:]
    return values.at[tuple(index_at)].set(least).at[tuple(beside)].set(high)


def shard_levels(key, dims, pieces, low, high):
    factor_of, own = 1.0, jax.random.fold_in(key, 6)
    for axis_at, blocks in pieces:
        draws = jnp.exp(jax.random.uniform(jax.random.fold_in(own, axis_at), (blocks,), jnp.float32, low / len(pieces), high / len(pieces)))
        factor_of = factor_of * jnp.repeat(draws, dims[axis_at] // blocks).reshape([-1 if axis == axis_at else 1 for axis in range(len(dims))])
    return factor_of


def noise(rng, shape, spread, most, pieces=(), held_as=jnp.bfloat16):
    entries = spread * jax.random.normal(rng, shape, jnp.float32)
    if pieces:
        entries = entries * shard_levels(rng, shape, pieces, -0.22, 0.18)
    return jnp.clip(entries, -most, most).astype(held_as)


def setup_inputs(seed: int = 0) -> dict:
    splits = jax.random.split(jax.random.key(seed), 14)
    queries = draw_queries(jax.random.fold_in(splits[13], 71), 0)
    new_kv = noise(splits[1], (KVH, TOKENS, 2 * HD), 2.5, 20.0, ((0, 4), (1, 64)))
    prefix_kv = draw_prefix_kv(jax.random.fold_in(splits[13], 71), 0)
    cache_kv = noise(splits[3], (KVH, POOL, PAGE, 2 * HD), 1.0, 6.0, ((0, 4), (1, 64)))
    page_table = jax.vmap(lambda own: jax.random.permutation(own, P_DEV))(jax.random.split(splits[4], N_REQ)).reshape((N_REQ, P_DEV)).astype(jnp.int32)
    page_counts = draw_page_counts(jax.random.fold_in(splits[13], 71), 0)
    cache_slack = set_ends(jax.random.randint(splits[6], (N_REQ, REQ_DEV), 0, PAGE), jax.random.fold_in(splits[6], 1), 0, PAGE - 1).astype(jnp.int32)
    parents = draw_parents(jax.random.fold_in(splits[13], 71), 0)
    tree_sizes = draw_tree_sizes(jax.random.fold_in(splits[13], 71), 0)
    accepted = draw_accepted(jax.random.fold_in(splits[13], 71), 0)
    out_weight = noise(splits[10], (HEADS * HD, D), HD ** -0.5, 0.5, ((0, 4),))
    residual = draw_residual(jax.random.fold_in(splits[13], 71), 0)
    norm_gain = jnp.clip(1.0 + 0.1 * jax.random.normal(splits[12], (D,), jnp.float32), 0.5, 1.5).astype(jnp.bfloat16)
    return dict(queries=queries, new_kv=new_kv, prefix_kv=prefix_kv, cache_kv=cache_kv, page_table=page_table, page_counts=page_counts, cache_slack=cache_slack, parents=parents, tree_sizes=tree_sizes, accepted=accepted, out_weight=out_weight, residual=residual, norm_gain=norm_gain)


MASKED_SCORE = -1e+30

def closure(parents):
    draft_len = parents.shape[1]
    slot_index = jnp.arange(draft_len, dtype=jnp.int32)
    parent_links = (parents[:, :, None] == slot_index[None, None, :]) & (slot_index[None, :, None] > 0)
    reached = jnp.eye(draft_len, dtype=jnp.float32)[None] + parent_links.astype(jnp.float32)
    for squaring in range((draft_len - 1).bit_length()):
        reached = jnp.minimum(jnp.einsum('rij,rjk->rik', reached, reached, precision=lax.Precision.HIGHEST), 1.0)
    return reached

def reference(queries, new_kv, prefix_kv, cache_kv, page_table, page_counts, cache_slack, parents, tree_sizes, accepted, out_weight, residual, norm_gain):
    group_size = HEADS // KVH
    starts = (jnp.cumsum(page_counts, axis=1) - page_counts).astype(jnp.int32)
    offsets = starts[:, :, None] + jnp.arange(MAXP, dtype=jnp.int32)[None, None, :]
    offsets = jnp.minimum(offsets, P_DEV - 1).astype(jnp.int32)
    device_index = jnp.arange(N_REQ, dtype=jnp.int32)[:, None, None]
    local_ids = page_table[device_index, offsets].astype(jnp.int32)
    global_ids = (local_ids + device_index * P_DEV).reshape(REQUESTS, MAXP).astype(jnp.int32)
    lengths = (page_counts * PAGE - cache_slack).reshape(REQUESTS).astype(jnp.int32)
    ancestors = closure(parents)
    tree_all = new_kv.reshape(KVH, REQUESTS, DRAFT, 2 * HD)
    query_all = queries.reshape(REQUESTS, DRAFT, KVH, group_size, HD)
    scaling = 1.0 / math.sqrt(HD)
    positions = jnp.arange(MAXP * PAGE, dtype=jnp.int32)
    slot_index = jnp.arange(DRAFT, dtype=jnp.int32)

    def one_request(index):
        page_rows = cache_kv[:, global_ids[index]].reshape(KVH, MAXP * PAGE, 2 * HD)
        tree_rows = lax.dynamic_index_in_dim(tree_all, index, 1, keepdims=False)
        key_rows = jnp.concatenate([prefix_kv[:, :, :HD], page_rows[:, :, :HD], tree_rows[:, :, :HD]], axis=1).astype(jnp.float32)
        value_rows = jnp.concatenate([prefix_kv[:, :, HD:], page_rows[:, :, HD:], tree_rows[:, :, HD:]], axis=1).astype(jnp.float32)
        query_rows = query_all[index].astype(jnp.float32)
        visible = jnp.concatenate([jnp.ones((DRAFT, PREFIX), dtype=bool), jnp.broadcast_to(positions[None, :] < lengths[index], (DRAFT, MAXP * PAGE)), ancestors[index] > 0.5], axis=1)
        scores = jnp.einsum('nkgh,kmh->kgnm', query_rows, key_rows) * scaling
        scores = jnp.where(visible[None, None], scores, MASKED_SCORE)
        largest = lax.optimization_barrier(jnp.max(scores, axis=-1, keepdims=True))
        weights = jnp.where(visible[None, None], jnp.exp(scores - largest), 0.0)
        totals = lax.optimization_barrier(jnp.sum(weights, axis=-1))
        rounded = lax.optimization_barrier(weights.astype(jnp.bfloat16)).astype(jnp.float32)
        mixture = jnp.einsum('kgnm,kmh->kgnh', rounded, value_rows)
        live = (slot_index < tree_sizes[index]).astype(jnp.float32)
        attended = mixture / totals[..., None] * live[None, None, :, None]
        return jnp.transpose(attended, (2, 0, 1, 3)).reshape(DRAFT, HEADS * HD).astype(jnp.bfloat16)
    attended = lax.map(one_request, jnp.arange(REQUESTS, dtype=jnp.int32)).reshape(TOKENS, HEADS * HD)
    projected = jnp.dot(attended, out_weight, preferred_element_type=jnp.float32)
    hidden_state = (residual.astype(jnp.float32) + projected).astype(jnp.bfloat16)
    widened = lax.optimization_barrier(hidden_state).astype(jnp.float32)
    meansq = lax.optimization_barrier(jnp.mean(widened * widened, axis=1, keepdims=True))
    normed_state = (widened * lax.rsqrt(meansq + 1e-05) * norm_gain.astype(jnp.float32)).astype(jnp.bfloat16)
    picked = (slot_index[None, :] == accepted[:, None]).astype(jnp.float32)
    on_path = jnp.einsum('ri,rij->rj', picked, ancestors, precision=lax.Precision.HIGHEST)
    placed = jnp.cumsum(on_path, axis=1) - 1.0
    compact = ((placed[:, None, :] == slot_index.astype(jnp.float32)[None, :, None]) & (on_path[:, None, :] > 0.5)).astype(jnp.float32)
    accepted_kv = jnp.einsum('rpj,krjc->krpc', compact, tree_all.astype(jnp.float32)).astype(jnp.bfloat16)
    return (hidden_state, normed_state, accepted_kv.reshape(KVH, TOKENS, 2 * HD))
```

```python
import math

import jax
import jax.numpy as jnp
from jax import lax
from jax.experimental import pallas as pl
from jax.experimental.pallas import tpu as pltpu
from jax.sharding import PartitionSpec as P

NX, NZ, NY = 4, 8, 2
HD = 128
GROUP = 4
TOK = 128
DRAFT = 64
PAGE = 128
CHUNK = 8
STAT = 16
SCALE = 1.0 / math.sqrt(HD)
NEG = -1e30


def spot(x, z, y):
    return (x % NX) * (NZ * NY) + (z % NZ) * NY + (y % NY)


def move(a, dx=0, dz=0, dy=0):
    pairs = [
        (spot(x, z, y), spot(x + dx, z + dz, y + dy))
        for x in range(NX)
        for z in range(NZ)
        for y in range(NY)
    ]
    return lax.ppermute(a, "req", pairs)


def swap_tp(a, bit):
    return lax.ppermute(a, "tp", [(i, i ^ bit) for i in range(4)])


def nt_dot(a, b):
    return lax.dot_general(a, b, (((1,), (1,)), ((), ())), preferred_element_type=jnp.float32)


def store_part(out_ref, at, heads_out, heads_lse):
    for g in range(GROUP):
        out_ref[at, :TOK, g * HD : (g + 1) * HD] = heads_out[g].astype(jnp.bfloat16)
    lane = lax.broadcasted_iota(jnp.int32, (TOK, HD), 1)
    spread = jnp.zeros((TOK, HD), jnp.float32)
    for g in range(GROUP):
        spread = jnp.where(lane == g, heads_lse[g], spread)
    flat = spread.T[:STAT]
    high = flat.astype(jnp.bfloat16)
    rest = flat - high.astype(jnp.float32)
    middle = rest.astype(jnp.bfloat16)
    low = (rest - middle.astype(jnp.float32)).astype(jnp.bfloat16)
    out_ref[at, TOK:, :HD] = high
    out_ref[at, TOK:, HD : 2 * HD] = middle
    out_ref[at, TOK:, 2 * HD : 3 * HD] = low
    out_ref[at, TOK:, 3 * HD :] = jnp.zeros_like(low)


def load_part(ref, at):
    stats = ref[at, TOK:, :].astype(jnp.float32)
    flat = stats[:, :HD] + stats[:, HD : 2 * HD] + stats[:, 2 * HD : 3 * HD]
    tall = jnp.concatenate([flat, jnp.zeros((HD - STAT, HD), jnp.float32)], axis=0).T
    outs = [ref[at, :TOK, g * HD : (g + 1) * HD].astype(jnp.float32) for g in range(GROUP)]
    return outs, [tall[:, g : g + 1] for g in range(GROUP)]


def merge(parts):
    outs, sums = [], []
    for g in range(GROUP):
        top = parts[0][1][g]
        for part in parts[1:]:
            top = jnp.maximum(top, part[1][g])
        total = jnp.zeros_like(top)
        acc = jnp.zeros((TOK, HD), jnp.float32)
        for part in parts:
            share = jnp.exp(part[1][g] - top)
            total = total + share
            acc = acc + share * part[0][g]
        outs.append(acc / total)
        sums.append(top + jnp.log(total))
    return outs, sums


def prefix_kernel(q_ref, *refs):
    kv_refs, out_ref = refs[:-1], refs[-1]
    outs, sums = [], []
    for half in range(2):
        first = 2 * half
        rows = jnp.concatenate(
            [q_ref[0, :, (first + g) * HD : (first + g + 1) * HD] for g in range(2)], axis=0
        )
        scores = [nt_dot(rows, ref[:, :HD]) for ref in kv_refs]
        top = jnp.max(scores[0], axis=1, keepdims=True)
        for s in scores[1:]:
            top = jnp.maximum(top, jnp.max(s, axis=1, keepdims=True))
        total = jnp.zeros_like(top)
        acc = jnp.zeros((2 * TOK, HD), jnp.float32)
        for s, ref in zip(scores, kv_refs):
            w = jnp.exp((s - top) * SCALE)
            total = total + jnp.sum(w, axis=1, keepdims=True)
            acc = acc + jnp.dot(
                w.astype(jnp.bfloat16), ref[:, HD:], preferred_element_type=jnp.float32
            )
        acc = acc / total
        lse = top * SCALE + jnp.log(total)
        for g in range(2):
            outs.append(acc[g * TOK : (g + 1) * TOK])
            sums.append(lse[g * TOK : (g + 1) * TOK])
    store_part(out_ref, 0, outs, sums)


def prefix_part(q, shards):
    whole = [pl.BlockSpec(s.shape, lambda i: (0, 0)) for s in shards]
    return pl.pallas_call(
        prefix_kernel,
        grid=(q.shape[0],),
        in_specs=[pl.BlockSpec((1, TOK, GROUP * HD), lambda i: (i, 0, 0))] + whole,
        out_specs=pl.BlockSpec((1, TOK + STAT, GROUP * HD), lambda i: (i, 0, 0)),
        out_shape=jax.ShapeDtypeStruct((q.shape[0], TOK + STAT, GROUP * HD), jnp.bfloat16),
        name="prefix_part",
    )(q, *shards)


def merge_kernel(*refs):
    out_ref = refs[-1]
    for b in range(2):
        outs, sums = merge([load_part(ref, b) for ref in refs[:-1]])
        store_part(out_ref, b, outs, sums)


def merge_parts(parts):
    return pl.pallas_call(
        merge_kernel,
        out_shape=jax.ShapeDtypeStruct(parts[0].shape, jnp.bfloat16),
        name="merge_parts",
    )(*parts)


def local_kernel(table_ref, counts_ref, slack_ref, q_ref, new_ref, anc_ref, *refs):
    pages = refs[:CHUNK]
    o_ref, lse_ref, top_ref, total_ref, acc_ref = refs[CHUNK:]
    step = pl.program_id(0)

    def rows_of(r):
        block = q_ref[r]
        return jnp.concatenate([block[:, g * HD : (g + 1) * HD] for g in range(GROUP)], axis=0)

    @pl.when(step == 0)
    def _():
        for r in range(2):
            s = nt_dot(rows_of(r), new_ref[r, :, :HD])
            seen = jnp.concatenate([anc_ref[r]] * GROUP, axis=0) > 0.5
            s = jnp.where(seen, s, NEG)
            top = jnp.max(s, axis=1, keepdims=True)
            w = jnp.where(seen, jnp.exp((s - top) * SCALE), 0.0)
            top_ref[r] = top
            total_ref[r] = jnp.sum(w, axis=1, keepdims=True)
            acc_ref[r] = jnp.dot(
                w.astype(jnp.bfloat16), new_ref[r, :, HD:], preferred_element_type=jnp.float32
            )

    first = counts_ref[0]
    r = (step * CHUNK >= first).astype(jnp.int32)
    length = counts_ref[r] * PAGE - slack_ref[r]
    start = (step * CHUNK - r * first) * PAGE
    rows = rows_of(r)
    lane = lax.broadcasted_iota(jnp.int32, (1, PAGE), 1)
    masks = [lane + (start + i * PAGE) < length for i in range(CHUNK)]
    scores = [
        jnp.where(masks[i], nt_dot(rows, pages[i][0, 0, :, :HD]), NEG) for i in range(CHUNK)
    ]
    peak = scores[0]
    for s in scores[1:]:
        peak = jnp.maximum(peak, s)
    old = top_ref[r]
    top = jnp.maximum(old, jnp.max(peak, axis=1, keepdims=True))
    factor = jnp.exp((old - top) * SCALE)
    run = jnp.zeros_like(peak)
    acc = acc_ref[r] * factor
    for i in range(CHUNK):
        w = jnp.where(masks[i], jnp.exp((scores[i] - top) * SCALE), 0.0)
        run = run + w
        acc = acc + jnp.dot(
            w.astype(jnp.bfloat16), pages[i][0, 0, :, HD:], preferred_element_type=jnp.float32
        )
    top_ref[r] = top
    total_ref[r] = total_ref[r] * factor + jnp.sum(run, axis=1, keepdims=True)
    acc_ref[r] = acc

    @pl.when(step == pl.num_programs(0) - 1)
    def _():
        for k in range(2):
            o = acc_ref[k] / total_ref[k]
            lse = top_ref[k] * SCALE + jnp.log(total_ref[k])
            for g in range(GROUP):
                here = slice(g * DRAFT, (g + 1) * DRAFT)
                o_ref[k * DRAFT : (k + 1) * DRAFT, g * HD : (g + 1) * HD] = o[here]
                lse_ref[g, k * DRAFT : (k + 1) * DRAFT, :] = lse[here]


def local_part(table, counts, slack, q, new_kv, anc, cache):
    def page_spec(i):
        return pl.BlockSpec(
            (1, 1, PAGE, 2 * HD), lambda s, table, counts, slack: (0, table[s * CHUNK + i], 0, 0)
        )

    rows = GROUP * DRAFT
    return pl.pallas_call(
        local_kernel,
        grid_spec=pltpu.PrefetchScalarGridSpec(
            num_scalar_prefetch=3,
            grid=(table.shape[0] // CHUNK,),
            in_specs=[
                pl.BlockSpec((2, DRAFT, GROUP * HD), lambda s, *_: (0, 0, 0)),
                pl.BlockSpec((2, DRAFT, 2 * HD), lambda s, *_: (0, 0, 0)),
                pl.BlockSpec((2, DRAFT, DRAFT), lambda s, *_: (0, 0, 0)),
            ]
            + [page_spec(i) for i in range(CHUNK)],
            out_specs=[
                pl.BlockSpec((TOK, GROUP * HD), lambda s, *_: (0, 0)),
                pl.BlockSpec((GROUP, TOK, 1), lambda s, *_: (0, 0, 0)),
            ],
            scratch_shapes=[
                pltpu.VMEM((2, rows, 1), jnp.float32),
                pltpu.VMEM((2, rows, 1), jnp.float32),
                pltpu.VMEM((2, rows, HD), jnp.float32),
            ],
        ),
        out_shape=[
            jax.ShapeDtypeStruct((TOK, GROUP * HD), jnp.float32),
            jax.ShapeDtypeStruct((GROUP, TOK, 1), jnp.float32),
        ],
        name="local_part",
    )(table, counts, slack, q, new_kv, anc, *([cache] * CHUNK))


def final_kernel(mine_ref, other_ref, o_ref, lse_ref, live_ref, out_ref):
    local = (
        [o_ref[:, g * HD : (g + 1) * HD] for g in range(GROUP)],
        [lse_ref[g] for g in range(GROUP)],
    )
    outs, _ = merge([load_part(mine_ref, 0), load_part(other_ref, 0), local])
    for g in range(GROUP):
        out_ref[:, g * HD : (g + 1) * HD] = (outs[g] * live_ref[...]).astype(jnp.bfloat16)


def closure(parents):
    slot_index = jnp.arange(DRAFT, dtype=jnp.int32)
    links = (parents[:, :, None] == slot_index[None, None, :]) & (slot_index[None, :, None] > 0)
    reached = (jnp.eye(DRAFT, dtype=jnp.float32)[None] + links.astype(jnp.float32)).astype(
        jnp.bfloat16
    )
    for _ in range((DRAFT - 1).bit_length()):
        reached = jnp.minimum(
            jnp.einsum("rij,rjk->rik", reached, reached, preferred_element_type=jnp.float32), 1.0
        ).astype(jnp.bfloat16)
    return reached.astype(jnp.float32)


def body(
    queries,
    new_kv,
    prefix_kv,
    cache_kv,
    page_table,
    page_counts,
    cache_slack,
    parents,
    tree_sizes,
    accepted,
    out_weight,
    residual,
    norm_gain,
):
    own = prefix_kv[0]
    shards = [own]
    up, down = own, own
    for _ in range(3):
        up, down = move(up, dz=1), move(down, dz=-1)
        shards += [up, down]
    half = own.shape[0] // 2
    shards += [move(up[:half], dz=1), move(down[half:], dz=-1)]
    pair = jnp.stack([queries, move(queries, dy=1)])
    shifts = (2, 1, -1)
    asked = [move(pair, dx=k) for k in shifts]

    ancestors = closure(parents)
    tree_rows = new_kv[0].reshape(2, DRAFT, 2 * HD)
    local_o, local_lse = local_part(
        page_table[0],
        page_counts[0],
        cache_slack[0],
        queries.reshape(2, DRAFT, GROUP * HD),
        tree_rows,
        ancestors,
        cache_kv,
    )

    slot_index = jnp.arange(DRAFT, dtype=jnp.int32)
    picked = (slot_index[None, :] == accepted[:, None]).astype(jnp.float32)
    on_path = jnp.sum(picked[:, :, None] * ancestors, axis=1)
    before = (slot_index[:, None] <= slot_index[None, :]).astype(jnp.float32)
    placed = jnp.sum(on_path[:, :, None] * before[None], axis=1) - 1.0
    compact = (
        (placed[:, None, :] == slot_index.astype(jnp.float32)[None, :, None])
        & (on_path[:, None, :] > 0.5)
    ).astype(jnp.bfloat16)
    accepted_kv = jnp.einsum(
        "rpj,rjc->rpc", compact, tree_rows, preferred_element_type=jnp.float32
    ).astype(jnp.bfloat16)

    replies = [move(prefix_part(q, shards), dx=-k) for q, k in zip(asked, shifts)]
    merged = merge_parts([prefix_part(pair, shards)] + replies)
    other = move(merged[1:], dy=1)
    live = (slot_index[None, :] < tree_sizes[:, None]).reshape(TOK, 1).astype(jnp.float32)
    attended = pl.pallas_call(
        final_kernel,
        out_shape=jax.ShapeDtypeStruct((TOK, GROUP * HD), jnp.bfloat16),
        name="final_part",
    )(merged[:1], other, local_o, local_lse, live)

    width = out_weight.shape[1]
    product = jnp.dot(attended, out_weight, preferred_element_type=jnp.float32)
    product = product.astype(jnp.bfloat16).reshape(2, 2, TOK // 4, width)
    at = lax.axis_index("tp")
    core, low = at % 2, at // 2
    kept = lax.dynamic_index_in_dim(product, core, 1, keepdims=False)
    sent = lax.dynamic_index_in_dim(product, 1 - core, 1, keepdims=False)
    twos = kept.astype(jnp.float32) + swap_tp(sent, 1).astype(jnp.float32)
    kept = lax.dynamic_index_in_dim(twos, low, 0, keepdims=False)
    sent = lax.dynamic_index_in_dim(twos, 1 - low, 0, keepdims=False).astype(jnp.bfloat16)
    summed = kept + swap_tp(sent, 2).astype(jnp.float32)
    hidden_state = (residual.astype(jnp.float32) + summed).astype(jnp.bfloat16)
    widened = lax.optimization_barrier(hidden_state).astype(jnp.float32)
    meansq = jnp.mean(widened * widened, axis=1, keepdims=True)
    normed_state = (widened * lax.rsqrt(meansq + 1e-05) * norm_gain.astype(jnp.float32)).astype(
        jnp.bfloat16
    )
    return (hidden_state, normed_state, accepted_kv.reshape(1, TOK, 2 * HD))


def solution(mesh):
    placed = (
        P("req", "tp"),
        P("tp", "req", None),
        P("tp", "req", None),
        P("tp", "req", None, None),
        P("req", None),
        P("req", None),
        P("req", None),
        P("req", None),
        P("req"),
        P("req"),
        P("tp", None),
        P(("req", "tp"), None),
        P(),
    )
    return jax.shard_map(
        body,
        mesh=mesh,
        in_specs=placed,
        out_specs=(P(("req", "tp"), None), P(("req", "tp"), None), P("tp", "req", None)),
        check_vma=False,
    )
```

```python
import math

import jax
import jax.numpy as jnp
from jax import lax
from jax.experimental import pallas as pl
from jax.experimental.pallas import tpu as pltpu
from jax.sharding import PartitionSpec as P


NX, NZ, NY = 4, 8, 2
HD = 128
GROUP = 4
TOK = 128
DRAFT = 64
PAGE = 128
CHUNK = 8
STAT = 16
KEYS = 256
SCALE = 1.0 / math.sqrt(HD)
NEG = -1e30


def spot(x, z, y):
    return (x % NX) * (NZ * NY) + (z % NZ) * NY + (y % NY)


def move(a, dx=0, dz=0, dy=0):
    pairs = [
        (spot(x, z, y), spot(x + dx, z + dz, y + dy))
        for x in range(NX)
        for z in range(NZ)
        for y in range(NY)
    ]
    return lax.ppermute(a, "req", pairs)


def swap_tp(a, bit):
    return lax.ppermute(a, "tp", [(i, i ^ bit) for i in range(4)])


def nt_dot(a, b):
    return lax.dot_general(a, b, (((1,), (1,)), ((), ())), preferred_element_type=jnp.float32)


def store_part(out_ref, at, heads_out, heads_lse):
    for g in range(GROUP):
        out_ref[at, :TOK, g * HD : (g + 1) * HD] = heads_out[g].astype(jnp.bfloat16)
    lane = lax.broadcasted_iota(jnp.int32, (TOK, HD), 1)
    spread = jnp.zeros((TOK, HD), jnp.float32)
    for g in range(GROUP):
        spread = jnp.where(lane == g, heads_lse[g], spread)
    flat = spread.T[:STAT]
    high = flat.astype(jnp.bfloat16)
    rest = flat - high.astype(jnp.float32)
    middle = rest.astype(jnp.bfloat16)
    low = (rest - middle.astype(jnp.float32)).astype(jnp.bfloat16)
    out_ref[at, TOK:, :HD] = high
    out_ref[at, TOK:, HD : 2 * HD] = middle
    out_ref[at, TOK:, 2 * HD : 3 * HD] = low
    out_ref[at, TOK:, 3 * HD :] = jnp.zeros_like(low)


def load_part(ref, at):
    stats = ref[at, TOK:, :].astype(jnp.float32)
    flat = stats[:, :HD] + stats[:, HD : 2 * HD] + stats[:, 2 * HD : 3 * HD]
    tall = jnp.concatenate([flat, jnp.zeros((HD - STAT, HD), jnp.float32)], axis=0).T
    outs = [ref[at, :TOK, g * HD : (g + 1) * HD].astype(jnp.float32) for g in range(GROUP)]
    return outs, [tall[:, g : g + 1] for g in range(GROUP)]


def merge(parts):
    outs, sums = [], []
    for g in range(GROUP):
        top = parts[0][1][g]
        for part in parts[1:]:
            top = jnp.maximum(top, part[1][g])
        total = jnp.zeros_like(top)
        acc = jnp.zeros((TOK, HD), jnp.float32)
        for part in parts:
            share = jnp.exp(part[1][g] - top)
            total = total + share
            acc = acc + share * part[0][g]
        outs.append(acc / total)
        sums.append(top + jnp.log(total))
    return outs, sums


def prefix_kernel(q_ref, *refs):
    out_ref = refs[-1]
    kv_refs = []
    for ref in refs[:-1]:
        kv_refs += [ref.at[pl.ds(k, KEYS)] for k in range(0, ref.shape[0], KEYS)]
    outs, sums = [], []
    for half in range(2):
        first = 2 * half
        rows = jnp.concatenate(
            [q_ref[0, :, (first + g) * HD : (first + g + 1) * HD] for g in range(2)], axis=0
        )
        scores = [nt_dot(rows, ref[:, :HD]) for ref in kv_refs]
        peak = scores[0]
        for s in scores[1:]:
            peak = jnp.maximum(peak, s)
        top = jnp.max(peak, axis=1, keepdims=True)
        run = jnp.zeros_like(peak)
        acc = jnp.zeros((2 * TOK, HD), jnp.float32)
        for s, ref in zip(scores, kv_refs):
            w = jnp.exp((s - top) * SCALE)
            run = run + w
            acc = acc + jnp.dot(
                w.astype(jnp.bfloat16), ref[:, HD:], preferred_element_type=jnp.float32
            )
        total = jnp.sum(run, axis=1, keepdims=True)
        acc = acc / total
        lse = top * SCALE + jnp.log(total)
        for g in range(2):
            outs.append(acc[g * TOK : (g + 1) * TOK])
            sums.append(lse[g * TOK : (g + 1) * TOK])
    store_part(out_ref, 0, outs, sums)


def prefix_part(q, shards):
    whole = [pl.BlockSpec(s.shape, lambda i: (0, 0)) for s in shards]
    return pl.pallas_call(
        prefix_kernel,
        grid=(q.shape[0],),
        in_specs=[pl.BlockSpec((1, TOK, GROUP * HD), lambda i: (i, 0, 0))] + whole,
        out_specs=pl.BlockSpec((1, TOK + STAT, GROUP * HD), lambda i: (i, 0, 0)),
        out_shape=jax.ShapeDtypeStruct((q.shape[0], TOK + STAT, GROUP * HD), jnp.bfloat16),
        name="prefix_part",
    )(q, *shards)


def merge_kernel(*refs):
    ins, out_refs = refs[:-2], refs[-2:]
    for b in range(2):
        outs, sums = merge([load_part(ref, b) for ref in ins])
        store_part(out_refs[b], 0, outs, sums)


def merge_parts(parts):
    one = jax.ShapeDtypeStruct((1,) + parts[0].shape[1:], jnp.bfloat16)
    return pl.pallas_call(merge_kernel, out_shape=[one, one], name="merge_parts")(*parts)


def local_kernel(table_ref, counts_ref, slack_ref, q_ref, new_ref, anc_ref, *refs):
    pages = refs[:CHUNK]
    o_ref, lse_ref, top_ref, total_ref, acc_ref = refs[CHUNK:]
    step = pl.program_id(0)

    def rows_of(r):
        block = q_ref[r]
        return jnp.concatenate([block[:, g * HD : (g + 1) * HD] for g in range(GROUP)], axis=0)

    @pl.when(step == 0)
    def _():
        for r in range(2):
            s = nt_dot(rows_of(r), new_ref[r, :, :HD])
            seen = jnp.concatenate([anc_ref[r]] * GROUP, axis=0) > 0.5
            s = jnp.where(seen, s, NEG)
            top = jnp.max(s, axis=1, keepdims=True)
            w = jnp.where(seen, jnp.exp((s - top) * SCALE), 0.0)
            top_ref[r] = top
            total_ref[r] = jnp.sum(w, axis=1, keepdims=True)
            acc_ref[r] = jnp.dot(
                w.astype(jnp.bfloat16), new_ref[r, :, HD:], preferred_element_type=jnp.float32
            )

    first = counts_ref[0]
    r = (step * CHUNK >= first).astype(jnp.int32)
    length = counts_ref[r] * PAGE - slack_ref[r]
    start = (step * CHUNK - r * first) * PAGE
    rows = rows_of(r)
    lane = lax.broadcasted_iota(jnp.int32, (1, PAGE), 1)
    masks = [lane + (start + i * PAGE) < length for i in range(CHUNK)]
    scores = [
        jnp.where(masks[i], nt_dot(rows, pages[i][0, 0, :, :HD]), NEG) for i in range(CHUNK)
    ]
    peak = scores[0]
    for s in scores[1:]:
        peak = jnp.maximum(peak, s)
    old = top_ref[r]
    top = jnp.maximum(old, jnp.max(peak, axis=1, keepdims=True))
    factor = jnp.exp((old - top) * SCALE)
    run = jnp.zeros_like(peak)
    acc = acc_ref[r] * factor
    for i in range(CHUNK):
        w = jnp.where(masks[i], jnp.exp((scores[i] - top) * SCALE), 0.0)
        run = run + w
        acc = acc + jnp.dot(
            w.astype(jnp.bfloat16), pages[i][0, 0, :, HD:], preferred_element_type=jnp.float32
        )
    top_ref[r] = top
    total_ref[r] = total_ref[r] * factor + jnp.sum(run, axis=1, keepdims=True)
    acc_ref[r] = acc

    @pl.when(step == pl.num_programs(0) - 1)
    def _():
        for k in range(2):
            o = acc_ref[k] / total_ref[k]
            lse = top_ref[k] * SCALE + jnp.log(total_ref[k])
            for g in range(GROUP):
                here = slice(g * DRAFT, (g + 1) * DRAFT)
                o_ref[k * DRAFT : (k + 1) * DRAFT, g * HD : (g + 1) * HD] = o[here]
                lse_ref[g, k * DRAFT : (k + 1) * DRAFT, :] = lse[here]


def local_part(table, counts, slack, q, new_kv, anc, cache):
    def page_spec(i):
        return pl.BlockSpec(
            (1, 1, PAGE, 2 * HD), lambda s, table, counts, slack: (0, table[s * CHUNK + i], 0, 0)
        )

    rows = GROUP * DRAFT
    return pl.pallas_call(
        local_kernel,
        grid_spec=pltpu.PrefetchScalarGridSpec(
            num_scalar_prefetch=3,
            grid=(table.shape[0] // CHUNK,),
            in_specs=[
                pl.BlockSpec((2, DRAFT, GROUP * HD), lambda s, *_: (0, 0, 0)),
                pl.BlockSpec((2, DRAFT, 2 * HD), lambda s, *_: (0, 0, 0)),
                pl.BlockSpec((2, DRAFT, DRAFT), lambda s, *_: (0, 0, 0)),
            ]
            + [page_spec(i) for i in range(CHUNK)],
            out_specs=[
                pl.BlockSpec((TOK, GROUP * HD), lambda s, *_: (0, 0)),
                pl.BlockSpec((GROUP, TOK, 1), lambda s, *_: (0, 0, 0)),
            ],
            scratch_shapes=[
                pltpu.VMEM((2, rows, 1), jnp.float32),
                pltpu.VMEM((2, rows, 1), jnp.float32),
                pltpu.VMEM((2, rows, HD), jnp.float32),
            ],
        ),
        out_shape=[
            jax.ShapeDtypeStruct((TOK, GROUP * HD), jnp.float32),
            jax.ShapeDtypeStruct((GROUP, TOK, 1), jnp.float32),
        ],
        name="local_part",
    )(table, counts, slack, q, new_kv, anc, *([cache] * CHUNK))


def final_kernel(mine_ref, other_ref, o_ref, lse_ref, live_ref, out_ref):
    local = (
        [o_ref[:, g * HD : (g + 1) * HD] for g in range(GROUP)],
        [lse_ref[g] for g in range(GROUP)],
    )
    outs, _ = merge([load_part(mine_ref, 0), load_part(other_ref, 0), local])
    for g in range(GROUP):
        out_ref[:, g * HD : (g + 1) * HD] = (outs[g] * live_ref[...]).astype(jnp.bfloat16)


def closure(parents):
    slot_index = jnp.arange(DRAFT, dtype=jnp.int32)
    links = (parents[:, :, None] == slot_index[None, None, :]) & (slot_index[None, :, None] > 0)
    reached = (jnp.eye(DRAFT, dtype=jnp.float32)[None] + links.astype(jnp.float32)).astype(
        jnp.bfloat16
    )
    for _ in range((DRAFT - 1).bit_length()):
        reached = jnp.minimum(
            jnp.einsum("rij,rjk->rik", reached, reached, preferred_element_type=jnp.float32), 1.0
        ).astype(jnp.bfloat16)
    return reached.astype(jnp.float32)


def body(
    queries,
    new_kv,
    prefix_kv,
    cache_kv,
    page_table,
    page_counts,
    cache_slack,
    parents,
    tree_sizes,
    accepted,
    out_weight,
    residual,
    norm_gain,
):
    own = prefix_kv[0]
    shards = [own]
    up, down = move(own, dz=1), move(own, dz=-1)
    across = move(own, dz=4)
    ups = move(jnp.concatenate([own, up]), dz=2)
    downs = move(jnp.concatenate([own, down]), dz=-2)
    shards = [own, up, down, ups, downs, across]
    pair = jnp.stack([queries, move(queries, dy=1)])
    shifts = (2, 1, -1)
    asked = []
    for k in shifts:
        asked.append(move(pair, dx=k))

    ancestors = closure(parents)
    tree_rows = new_kv[0].reshape(2, DRAFT, 2 * HD)
    local_o, local_lse = local_part(
        page_table[0],
        page_counts[0],
        cache_slack[0],
        queries.reshape(2, DRAFT, GROUP * HD),
        tree_rows,
        ancestors,
        cache_kv,
    )

    slot_index = jnp.arange(DRAFT, dtype=jnp.int32)
    picked = (slot_index[None, :] == accepted[:, None]).astype(jnp.float32)
    on_path = jnp.sum(picked[:, :, None] * ancestors, axis=1)
    before = (slot_index[:, None] <= slot_index[None, :]).astype(jnp.float32)
    placed = jnp.sum(on_path[:, :, None] * before[None], axis=1) - 1.0
    compact = (
        (placed[:, None, :] == slot_index.astype(jnp.float32)[None, :, None])
        & (on_path[:, None, :] > 0.5)
    ).astype(jnp.bfloat16)
    accepted_kv = jnp.einsum(
        "rpj,rjc->rpc", compact, tree_rows, preferred_element_type=jnp.float32
    ).astype(jnp.bfloat16)

    replies = [move(prefix_part(q, shards), dx=-k) for q, k in zip(asked, shifts)]
    mine, theirs = merge_parts([prefix_part(pair, shards)] + replies)
    other = move(theirs, dy=1)
    live = (slot_index[None, :] < tree_sizes[:, None]).reshape(TOK, 1).astype(jnp.float32)
    attended = pl.pallas_call(
        final_kernel,
        out_shape=jax.ShapeDtypeStruct((TOK, GROUP * HD), jnp.bfloat16),
        name="final_part",
    )(mine, other, local_o, local_lse, live)

    width = out_weight.shape[1]
    product = jnp.dot(attended, out_weight, preferred_element_type=jnp.float32)
    product = product.astype(jnp.bfloat16).reshape(2, 2, TOK // 4, width)
    at = lax.axis_index("tp")
    core, low = at % 2, at // 2
    kept = lax.dynamic_index_in_dim(product, core, 1, keepdims=False)
    sent = lax.dynamic_index_in_dim(product, 1 - core, 1, keepdims=False)
    twos = kept.astype(jnp.float32) + swap_tp(sent, 1).astype(jnp.float32)
    kept = lax.dynamic_index_in_dim(twos, low, 0, keepdims=False)
    sent = lax.dynamic_index_in_dim(twos, 1 - low, 0, keepdims=False).astype(jnp.bfloat16)
    summed = kept + swap_tp(sent, 2).astype(jnp.float32)
    hidden_state = (residual.astype(jnp.float32) + summed).astype(jnp.bfloat16)
    widened = lax.optimization_barrier(hidden_state).astype(jnp.float32)
    meansq = jnp.mean(widened * widened, axis=1, keepdims=True)
    normed_state = (widened * lax.rsqrt(meansq + 1e-05) * norm_gain.astype(jnp.float32)).astype(
        jnp.bfloat16
    )
    return (hidden_state, normed_state, accepted_kv.reshape(1, TOK, 2 * HD))


def solution(mesh):
    placed = (
        P("req", "tp"),
        P("tp", "req", None),
        P("tp", "req", None),
        P("tp", "req", None, None),
        P("req", None),
        P("req", None),
        P("req", None),
        P("req", None),
        P("req"),
        P("req"),
        P("tp", None),
        P(("req", "tp"), None),
        P(),
    )

    return jax.shard_map(
        body,
        mesh=mesh,
        in_specs=placed,
        out_specs=(P(("req", "tp"), None), P(("req", "tp"), None), P("tp", "req", None)),
        check_vma=False,
    )
```
